256 devices in a mesh: row: 32 (over z, x_hi, core), col: 8 (over x_lo, y).
Axes of the slice: x: 4 (x_hi: 2, x_lo: 2; x = x_hi * 2 + x_lo), y: 4, z: 8, core: 2. Of those that a mesh axis runs over, the one named last changes fastest.
Arguments:
- tokens: bfloat16 [2048, 12288], P('col', 'row'), may hold values from -6 to 6
- weight: bfloat16 [12288, 24576], P('row', 'col'), may hold values from -0.0546875 to 0.0546875
- pre_act: bfloat16 [2048, 24576], P('row', 'col'), may hold values from -6 to 6
- out_grad: bfloat16 [2048, 24576], P('row', 'col'), may hold values from -6 to 6
Outputs:
- input_grad: bfloat16 [2048, 12288], P('col', 'row')
- weight_grad: bfloat16 [12288, 24576], P('row', 'col')
- left_stats: bfloat16 [12288, 24576], P('row', 'col')
- right_stats: bfloat16 [12288, 24576], P('row', 'col')
The draws below stay inside these ranges and needn't reach their ends.
All inputs are finite; a program needn't handle non-finite values.
Results may differ from the reference program's by a relative error of at most 0.0054.
Values may be sent and summed in bfloat16 or wider, within the bound.
A program may use at most 128 MiB of HBM per device.

```python
import math
import jax
import jax.numpy as jnp
from jax import lax

D = 12288
FF = 24576
BLOCK = 384
TOKENS = 2048


def level_of(own_key, shape, split, least, largest):
    level, own = 1.0, jax.random.fold_in(own_key, 6)
    for axis_at, shards_of in split:
        steps = jnp.exp(jax.random.uniform(jax.random.fold_in(own, axis_at), (shards_of,), jnp.float32, least / len(split), largest / len(split)))
        level = level * jnp.repeat(steps, shape[axis_at] // shards_of).reshape([-1 if axis == axis_at else 1 for axis in range(len(shape))])
    return level


def bell_draw(own_key, shape, scale, most, shards=(), kind=jnp.bfloat16):
    drawn = scale * jax.random.normal(own_key, shape, jnp.float32)
    if shards:
        drawn = drawn * level_of(own_key, shape, shards, -0.22, 0.18)
    return jnp.clip(drawn, -most, most).astype(kind)


def setup_inputs(seed: int = 0) -> dict:
    streams_of = jax.random.split(jax.random.key(seed), 5)
    tokens = bell_draw(streams_of[0], (TOKENS, D), 1.0, 6.0, ((0, 8), (1, 32)))
    weight = bell_draw(streams_of[1], (D, FF), D ** -0.5, 0.0546875, ((0, 32), (1, 8)))
    pre_act = bell_draw(streams_of[2], (TOKENS, FF), 1.0, 6.0, ((0, 32), (1, 8)))
    out_grad = bell_draw(streams_of[3], (TOKENS, FF), 1.0, 6.0, ((0, 32), (1, 8)))
    return {"tokens": tokens, "weight": weight, "pre_act": pre_act, "out_grad": out_grad}


def gelu_slope(value):
    coeff = math.sqrt(2.0 / math.pi)
    inner = coeff * (value + 0.044715 * value * value * value)
    tanh_u = jnp.tanh(inner)
    return 0.5 * (1.0 + tanh_u) + 0.5 * value * (1.0 - tanh_u * tanh_u) * coeff * (1.0 + 3.0 * 0.044715 * value * value)

def reference(tokens, weight, pre_act, out_grad):
    num_tokens = tokens.shape[0]
    scale = 1.0 / (BLOCK * num_tokens)

    def one_block(carry, index):
        start = index * BLOCK
        h_blk = lax.dynamic_slice_in_dim(pre_act, start, BLOCK, 1).astype(jnp.float32)
        g_blk = lax.dynamic_slice_in_dim(out_grad, start, BLOCK, 1).astype(jnp.float32)
        hidden_grad = (g_blk * gelu_slope(h_blk)).astype(jnp.bfloat16)
        w_blk = lax.dynamic_slice_in_dim(weight, start, BLOCK, 1)
        carry = carry + lax.dot_general(hidden_grad, w_blk, (((1,), (1,)), ((), ())), preferred_element_type=jnp.float32)
        weight_sum = lax.dot_general(tokens, hidden_grad, (((0,), (0,)), ((), ())), preferred_element_type=jnp.float32)
        tiles = weight_sum.reshape(D // BLOCK, BLOCK, BLOCK)
        left = jnp.einsum('ipq,irq->ipr', tiles, tiles, precision=lax.Precision.HIGHEST) * scale
        right = jnp.einsum('ipq,ipr->iqr', tiles, tiles, precision=lax.Precision.HIGHEST) * scale
        return (carry, (weight_sum.astype(jnp.bfloat16), left.reshape(D, BLOCK).astype(jnp.bfloat16), right.reshape(D, BLOCK).astype(jnp.bfloat16)))
    init = jnp.zeros((num_tokens, D), jnp.float32)
    indices = jnp.arange(FF // BLOCK, dtype=jnp.int32)
    summed, (grads, lefts, rights) = lax.scan(one_block, init, indices)

    def place(stacked):
        return jnp.transpose(stacked, (1, 0, 2)).reshape(D, FF)
    return (summed.astype(jnp.bfloat16), place(grads), place(lefts), place(rights))
```

```python
import functools
import math

import jax
import jax.numpy as jnp
from jax import lax
from jax.experimental import pallas as pl
from jax.experimental.pallas import tpu as pltpu
from jax.sharding import PartitionSpec as P

MESH = pl.DeviceIdType.MESH
BF, F32 = jnp.bfloat16, jnp.float32
BLOCK = 384
LATE = 2
NT = (((1,), (1,)), ((), ()))
NN = (((1,), (0,)), ((), ()))
DIST = (0, 1, 7, 2, 6, 3, 5, 4)
GROUPS = ((0, 768, False), (768, 768, True), (1536, 768, False), (2304, 768, True))
PHASES = ((0, 1), (2, 3))
HALF = 1536


def gelu_slope(value):
    coeff = math.sqrt(2.0 / math.pi)
    inner = coeff * (value + 0.044715 * value * value * value)
    tanh_u = jnp.tanh(inner)
    return 0.5 * (1.0 + tanh_u) + 0.5 * value * (1.0 - tanh_u * tanh_u) * coeff * (
        1.0 + 3.0 * 0.044715 * value * value
    )


def mm(a, b, dims=NN):
    return lax.dot_general(a, b, dims, preferred_element_type=F32)


def statistics(g, scale):
    hi = g.astype(BF)
    lo = (g - hi.astype(F32)).astype(BF)
    hi_t, lo_t = hi.T, lo.T
    a = mm(hi, lo_t)
    left = mm(hi, hi_t) + (a + a.T)
    b = mm(hi_t, lo)
    right = mm(hi_t, hi) + (b + b.T)
    return hi, (left * scale).astype(BF), (right * scale).astype(BF)


def slot_of(d):
    far = d // 5
    return (1 - far) * (2 * d - 1) + far * (16 - 2 * d) + (7 - d) // 7


def kernel(scale, early, tok_in, wt_in, pre_in, og_in, done_out, rest_out, dx_out,
           hid, wt, pre, og, tok_raw, tok_own, tok, dxacc, dxs, dxr, xs, xr, dxo, dw, outs,
           lsem, rsem, bsem, tsem, dsem, xsem, zs_sem, xs_sem, bs_sem, ts_sem, ds_sem, os_sem):
    r = lax.axis_index("row")
    c = lax.axis_index("col")
    core = r % 2
    xh = (r // 2) % 2
    z = r // 4
    xl = c // 4
    y = c % 4

    def row_id(zz, hh, cc):
        return (zz * 2 + hh) * 2 + cc

    sib = (row_id(z, xh, 1 - core), c)
    up = (row_id((z + 1) % 8, xh, core), c)
    down = (row_id((z + 7) % 8, xh, core), c)
    last = (row_id((z + 1 + 6 * core) % 8, xh, core), c)
    across = (row_id(z, 1 - xh, core), c)
    xpeer = (r, (1 - xl) * 4 + y)
    ypeer = [None] + [(r, xl * 4 + (y + j) % 4) for j in (1, 2, 3)]

    bar = pltpu.get_barrier_semaphore()
    peers = [sib, up, down, across, xpeer] + ypeer[1:]
    for peer in peers:
        pl.semaphore_signal(bar, inc=1, device_id=peer, device_id_type=MESH)

    loads = [
        pltpu.make_async_copy(pre_in, pre, lsem.at[0]),
        pltpu.make_async_copy(og_in, og, lsem.at[1]),
        pltpu.make_async_copy(tok_in, tok_raw, lsem.at[2]),
        pltpu.make_async_copy(wt_in, wt, lsem.at[3]),
    ]
    for cp in loads:
        cp.start()

    rows_of = [pl.multiple_of((xh * 2 + core) * 64, 64), pl.multiple_of(((1 - xh) * 2 + core) * 64, 64)]
    sib_rows = [pl.multiple_of((xh * 2 + 1 - core) * 64, 64), pl.multiple_of(((1 - xh) * 2 + 1 - core) * 64, 64)]

    def piece(g, slot, rows):
        return hid.at[slot, pl.ds(rows, 64), pl.ds(GROUPS[g][0], GROUPS[g][1])]

    sent = []

    def push(src, dst, send_sem, recv_sem, to):
        cp = pltpu.make_async_remote_copy(src_ref=src, dst_ref=dst, send_sem=send_sem, recv_sem=recv_sem,
                                          device_id=to, device_id_type=MESH)
        cp.start()
        sent.append(cp)

    def arrived(dst, recv_sem, frm):
        pltpu.make_async_remote_copy(src_ref=dst, dst_ref=dst, send_sem=lsem.at[7], recv_sem=recv_sem,
                                     device_id=frm, device_id_type=MESH).wait_recv()

    def push_z(g, p, src, dst, to):
        push(piece(g, src, rows_of[p]), piece(g, dst, rows_of[p]), zs_sem.at[g, p, dst], rsem.at[g, p, dst], to)

    def forward(g, p, slot):
        once = GROUPS[g][2]
        if p == 0 and once and slot == 0:
            push(piece(g, 0, rows_of[0]), piece(g, 0, rows_of[0]), xs_sem.at[g, 0], rsem.at[g, 1, 0], across)
        if p == 0 or once:
            if slot in (0, 1, 3):
                push_z(g, p, slot, slot + 2 if slot else 1, down)
            if slot in (0, 2, 4):
                push_z(g, p, slot, slot + 2, up)
        if p == 0 and not once:
            push(piece(g, slot, rows_of[0]), piece(g, slot, rows_of[0]), xs_sem.at[g, slot], rsem.at[g, 1, slot],
                 across)
        push(piece(g, slot, rows_of[p]), piece(g, slot, rows_of[p]), bs_sem.at[g, p, slot], bsem.at[g, p, slot], sib)

    def got(g, p, slots):
        frm = across if p == 1 else up
        for slot in slots:
            arrived(piece(g, slot, rows_of[p]), rsem.at[g, p, slot], frm)
            forward(g, p, slot)
        if 5 in slots and (p == 0 or GROUPS[g][2]):
            push_z(g, p, 6 - core, 7, last)

    def sibling(phase, slots):
        for slot in slots:
            for g in PHASES[phase]:
                for p in (0, 1):
                    arrived(piece(g, slot, sib_rows[p]), bsem.at[g, p, slot], sib)

    def hidden(phase):
        for k in range(4):
            cols = pl.ds(phase * HALF + k * BLOCK, BLOCK)
            val = og[:, cols].astype(F32) * gelu_slope(pre[:, cols].astype(F32))
            hid[0, pl.ds(rows_of[0], 64), cols] = val.astype(BF)

    def dx_task(phase, first, n):
        cols = pl.ds(phase * HALF, HALF)
        val = mm(hid[pl.ds(first, n), :, cols].reshape(n * 256, HALF), wt[:, cols], NT)
        val = val.reshape(n, 256, BLOCK)
        if phase == 0:
            dxacc[pl.ds(first, n)] = val
        else:
            val = val + dxacc[pl.ds(first, n)]
            dxacc[pl.ds(first, n)] = val
            dxs[pl.ds(first, n)] = val.astype(BF)

    def dx_send(slots):
        for slot in slots:
            t = (z + DIST[slot]) % 8
            to_x, to_y = t // 4, t % 4
            j = (to_y + 4 - y) % 4

            @pl.when(j != 0)
            def _():
                pltpu.make_async_remote_copy(
                    src_ref=dxs.at[slot], dst_ref=dxr.at[to_x, j], send_sem=ds_sem.at[slot],
                    recv_sem=dsem.at[to_x, j], device_id=(r, xl * 4 + to_y), device_id_type=MESH).start()

    def dw_all(phase, k):
        cols = pl.ds(phase * HALF + k * 768, 768)
        dw[:, cols] = mm(tok[...], hid[:, :, cols].reshape(2048, 768))

    def dw_part(first, n, fresh):
        for k in range(2):
            cols = pl.ds(HALF + k * 768, 768)
            val = mm(tok[:, pl.ds(first * 256, n * 256)], hid[pl.ds(first, n), :, cols].reshape(n * 256, 768))
            dw[:, cols] = val if fresh else dw[:, cols] + val

    pending = []
    written = []

    def flush():
        for b in pending:
            cp = pltpu.make_async_copy(outs.at[:, :, pl.ds(b * BLOCK, BLOCK)],
                                       done_out.at[:, :, pl.ds(b * BLOCK, BLOCK)], os_sem.at[b])
            cp.start()
            written.append(cp)
        pending.clear()

    def stats(b):
        flush()
        cols = pl.ds(b * BLOCK, BLOCK)
        grad, left, right = statistics(dw[:, cols], scale)
        outs[0, :, cols] = grad
        outs[1, :, cols] = left
        outs[2, :, cols] = right
        pending.append(b)

    loads[0].wait()
    loads[1].wait()
    hidden(0)
    loads[2].wait()
    tok_own[...] = tok_raw[...].T
    pl.semaphore_wait(bar, len(peers))

    def own(phase):
        g_every, g_once = PHASES[phase]
        push(piece(g_once, 0, rows_of[0]), piece(g_once, 0, rows_of[0]), xs_sem.at[g_once, 0], rsem.at[g_once, 1, 0],
             across)
        for g in PHASES[phase]:
            push_z(g, 0, 0, 1, down)
            push_z(g, 0, 0, 2, up)
        push(piece(g_every, 0, rows_of[0]), piece(g_every, 0, rows_of[0]), xs_sem.at[g_every, 0],
             rsem.at[g_every, 1, 0], across)
        for g in PHASES[phase]:
            push(piece(g, 0, rows_of[0]), piece(g, 0, rows_of[0]), bs_sem.at[g, 0, 0], bsem.at[g, 0, 0], sib)

    own(0)

    def tok_at(col):
        return tok.at[:, pl.ds(pl.multiple_of(slot_of((col + 8 - z) % 8) * 256, 256), 256)]

    push(tok_own, tok_at(c), ts_sem.at[0, 0], tsem.at[0, 0], xpeer)
    for j in (1, 2, 3):
        push(tok_own, tok_at(c), ts_sem.at[0, j], tsem.at[0, j], ypeer[j])
    keep = pltpu.make_async_copy(tok_own, tok_at(c), lsem.at[4])
    keep.start()
    hidden(1)
    loads[3].wait()

    def tok_relay():
        other = (1 - xl) * 4 + y
        arrived(tok_at(other), tsem.at[0, 0], xpeer)
        for j in (1, 2, 3):
            push(tok_at(other), tok_at(other), ts_sem.at[1, j], tsem.at[1, j], ypeer[j])

    def tok_wait():
        keep.wait()
        for j in (1, 2, 3):
            src_y = (y + 4 - j) % 4
            arrived(tok_at(xl * 4 + src_y), tsem.at[0, j], ypeer[j])
            arrived(tok_at((1 - xl) * 4 + src_y), tsem.at[1, j], ypeer[j])

    fill = [lambda: (tok_wait(), dw_all(0, 0)), lambda: dw_all(0, 1)] + [functools.partial(stats, b) for b in range(4)]

    def filler(phase, n=1):
        if phase:
            for _ in range(n):
                if fill:
                    fill.pop(0)()

    def near(phase, s):
        first, n = (0, 1) if s == 0 else (7, 1) if s == 4 else (2 * s - 1, 2)
        sibling(phase, range(first, first + n))
        dx_task(phase, first, n)
        return first, n

    for phase in (0, 1):
        every, once = PHASES[phase]
        for s in (1, 2, 3, 4):
            now = (7,) if s == 4 else (2 * s - 1, 2 * s)
            before = (0,) if s == 1 else (2 * s - 3, 2 * s - 2)
            if s == 4 and phase == 0:
                own(1)
            got(every, 0, now)
            filler(phase)
            got(once, 1, before)
            filler(phase)
            got(once, 0, now)
            got(every, 1, before)
            if phase == 0 and s == 1:
                tok_relay()
            first, n = near(phase, s - 1)
            if phase:
                dw_part(first, n, s == 1)
                dx_send(range(first, first + n))
        got(once, 1, (7,))
        filler(phase)
        got(every, 1, (7,))
        near(phase, 4)
        if phase:
            filler(phase, 9)
            dx_send((7,))
            dw_part(7, 1, False)

    rest = pltpu.make_async_copy(dw.at[:, pl.ds(early * BLOCK, (8 - early) * BLOCK)], rest_out, lsem.at[5])
    for b in range(4, early):
        stats(b)
    rest.start()

    def total(at_x):
        t = at_x * 4 + y
        val = dxacc[slot_of((t + 8 - z) % 8)]
        for j in (1, 2, 3):
            arrived(dxr.at[at_x, j], dsem.at[at_x, j], ypeer[j])
            val = val + dxr[at_x, j].astype(F32)
        return val

    xs[...] = total(1 - xl).astype(BF)
    flush()
    dxo_mine = total(xl)
    push(xs, xr, xsem.at[0], xsem.at[1], xpeer)
    arrived(xr, xsem.at[1], xpeer)
    dxo[...] = (dxo_mine + xr[...].astype(F32)).astype(BF)
    out = pltpu.make_async_copy(dxo, dx_out, lsem.at[6])
    out.start()
    for cp in sent:
        cp.wait_send()
    for slot in range(8):
        t = (z + DIST[slot]) % 8

        @pl.when((t % 4 + 4 - y) % 4 != 0)
        def _():
            pltpu.make_async_remote_copy(
                src_ref=dxs.at[slot], dst_ref=dxr.at[0, 1], send_sem=ds_sem.at[slot],
                recv_sem=dsem.at[0, 1], device_id=xpeer, device_id_type=MESH).wait_send()

    for cp in written:
        cp.wait()
    rest.wait()
    out.wait()


def finish(scale, early, done_in, rest_in, dx_in, gw_out, left_out, right_out, dx_out,
           done, rest, outs, dxv, isem, osem, rsem):
    late = 8 - early
    cps = [pltpu.make_async_copy(rest_in, rest, rsem), pltpu.make_async_copy(dx_in, dxv, isem.at[3])]
    cps += [pltpu.make_async_copy(done_in.at[i], done.at[i], isem.at[i]) for i in range(3)]
    for cp in cps:
        cp.start()
    hbm = (gw_out, left_out, right_out)
    res = []

    def put(src, dst, sem):
        cp = pltpu.make_async_copy(src, dst, sem)
        cp.start()
        res.append(cp)

    cps[0].wait()
    for k in range(late):
        cols = pl.ds(k * BLOCK, BLOCK)
        vals = statistics(rest[:, cols], scale)
        for i in range(3):
            outs[i, :, cols] = vals[i]
        if k == 0:
            for i in range(3):
                cps[2 + i].wait()
                put(done.at[i], hbm[i].at[:, pl.ds(0, early * BLOCK)], osem.at[8, i])
        for i in range(3):
            put(outs.at[i, :, cols], hbm[i].at[:, pl.ds((early + k) * BLOCK, BLOCK)], osem.at[k, i])
    cps[1].wait()
    put(dxv, dx_out, isem.at[4])
    for cp in res:
        cp.wait()


def on_device(tokens, weight, pre_act, out_grad):
    early = 8 - LATE
    scale = 1.0 / (BLOCK * 2048)
    anyspec = pl.BlockSpec(memory_space=pl.ANY)
    dma, vmem = pltpu.SemaphoreType.DMA, pltpu.VMEM
    done, rest, dx = pl.pallas_call(
        functools.partial(kernel, scale, early),
        out_shape=(
            jax.ShapeDtypeStruct((3, BLOCK, early * BLOCK), BF),
            jax.ShapeDtypeStruct((BLOCK, LATE * BLOCK), F32),
            jax.ShapeDtypeStruct((256, BLOCK), BF),
        ),
        in_specs=[anyspec] * 4,
        out_specs=(anyspec,) * 3,
        scratch_shapes=[
            vmem((8, 256, 3072), BF), vmem((BLOCK, 3072), BF), vmem((64, 3072), BF), vmem((64, 3072), BF),
            vmem((256, BLOCK), BF), vmem((BLOCK, 256), BF), vmem((BLOCK, 2048), BF),
            vmem((8, 256, BLOCK), F32), vmem((8, 256, BLOCK), BF), vmem((2, 4, 256, BLOCK), BF),
            vmem((256, BLOCK), BF), vmem((256, BLOCK), BF), vmem((256, BLOCK), BF),
            vmem((BLOCK, 3072), F32), vmem((3, BLOCK, early * BLOCK), BF),
            dma((8,)), dma((4, 2, 8)), dma((4, 2, 8)), dma((2, 4)), dma((2, 4)), dma((2,)),
            dma((4, 2, 8)), dma((4, 8)), dma((4, 2, 8)), dma((2, 4)), dma((8,)), dma((8,)),
        ],
        compiler_params=pltpu.CompilerParams(collective_id=0, has_side_effects=True,
                                             vmem_limit_bytes=60 * 2**20),
        name="exchange",
    )(tokens, weight, pre_act, out_grad)
    full = jax.ShapeDtypeStruct((BLOCK, 3072), BF)
    gw, left, right, dx = pl.pallas_call(
        functools.partial(finish, scale, early),
        out_shape=(full, full, full, jax.ShapeDtypeStruct((256, BLOCK), BF)),
        in_specs=[anyspec] * 3,
        out_specs=(anyspec,) * 4,
        scratch_shapes=[
            vmem((3, BLOCK, early * BLOCK), BF), vmem((BLOCK, LATE * BLOCK), F32), vmem((3, BLOCK, LATE * BLOCK), BF),
            vmem((256, BLOCK), BF), dma((5,)), dma((9, 3)), dma,
        ],
        compiler_params=pltpu.CompilerParams(vmem_limit_bytes=32 * 2**20),
        name="finish",
    )(done, rest, dx)
    return dx, gw, left, right


def solution(mesh):
    specs = (P("col", "row"), P("row", "col"), P("row", "col"), P("row", "col"))
    return jax.shard_map(on_device, mesh=mesh, in_specs=specs, out_specs=specs, check_vma=False)
```

```python
import functools
import math

import jax
import jax.numpy as jnp
from jax import lax
from jax.experimental import pallas as pl
from jax.experimental.pallas import tpu as pltpu
from jax.sharding import PartitionSpec as P

MESH = pl.DeviceIdType.MESH
BF, F32 = jnp.bfloat16, jnp.float32
BLOCK = 384
LATE = 2
NT = (((1,), (1,)), ((), ()))
NN = (((1,), (0,)), ((), ()))
DIST = (0, 1, 7, 2, 6, 3, 5, 4)
W = 768
NB = 3072 // W
NONCE = (NB // 4, NB // 4)
GROUPS = tuple((g * W, W, g % (NB // 2) >= NB // 2 - NONCE[g // (NB // 2)]) for g in range(NB))
PHASES = (tuple(range(NB // 2)), tuple(range(NB // 2, NB)))
ONCE = tuple(tuple(g for g in ph if GROUPS[g][2]) for ph in PHASES)
EVERY = tuple(tuple(g for g in ph if not GROUPS[g][2]) for ph in PHASES)
LEVEL = ((0,), (1, 2), (3, 4), (5, 6), (7,))
LAG = 1
LAG2 = 1
OWN2 = 4
FILL_N = 2
HALF = 1536


def gelu_slope(value):
    coeff = math.sqrt(2.0 / math.pi)
    inner = coeff * (value + 0.044715 * value * value * value)
    tanh_u = jnp.tanh(inner)
    return 0.5 * (1.0 + tanh_u) + 0.5 * value * (1.0 - tanh_u * tanh_u) * coeff * (
        1.0 + 3.0 * 0.044715 * value * value
    )


def mm(a, b, dims=NN):
    return lax.dot_general(a, b, dims, preferred_element_type=F32)


def statistics(g, scale):
    hi = g.astype(BF)
    lo = (g - hi.astype(F32)).astype(BF)
    hi_t, lo_t = hi.T, lo.T
    a = mm(hi, lo_t)
    left = mm(hi, hi_t) + (a + a.T)
    b = mm(hi_t, lo)
    right = mm(hi_t, hi) + (b + b.T)
    return hi, (left * scale).astype(BF), (right * scale).astype(BF)


def slot_of(d):
    far = d // 5
    return (1 - far) * (2 * d - 1) + far * (16 - 2 * d) + (7 - d) // 7


def kernel(scale, early, tok_in, wt_in, pre_in, og_in, done_out, rest_out, dx_out,
           hid, wt, pre, og, tok_raw, tok_own, tok, dxacc, dxs, dxr, xs, xr, dxo, dw, outs,
           lsem, rsem, bsem, tsem, dsem, xsem, zs_sem, xs_sem, bs_sem, ts_sem, ds_sem, os_sem):
    r = lax.axis_index("row")
    c = lax.axis_index("col")
    core = r % 2
    xh = (r // 2) % 2
    z = r // 4
    xl = c // 4
    y = c % 4

    def row_id(zz, hh, cc):
        return (zz * 2 + hh) * 2 + cc

    sib = (row_id(z, xh, 1 - core), c)
    up = (row_id((z + 1) % 8, xh, core), c)
    down = (row_id((z + 7) % 8, xh, core), c)
    last = (row_id((z + 1 + 6 * core) % 8, xh, core), c)
    across = (row_id(z, 1 - xh, core), c)
    xpeer = (r, (1 - xl) * 4 + y)
    ypeer = [None] + [(r, xl * 4 + (y + j) % 4) for j in (1, 2, 3)]

    bar = pltpu.get_barrier_semaphore()
    peers = [sib, up, down, across, xpeer] + ypeer[1:]
    for peer in peers:
        pl.semaphore_signal(bar, inc=1, device_id=peer, device_id_type=MESH)

    loads = [
        pltpu.make_async_copy(pre_in, pre, lsem.at[0]),
        pltpu.make_async_copy(og_in, og, lsem.at[1]),
        pltpu.make_async_copy(tok_in, tok_raw, lsem.at[2]),
        pltpu.make_async_copy(wt_in, wt, lsem.at[3]),
    ]
    for cp in loads:
        cp.start()

    rows_of = [pl.multiple_of((xh * 2 + core) * 64, 64), pl.multiple_of(((1 - xh) * 2 + core) * 64, 64)]
    sib_rows = [pl.multiple_of((xh * 2 + 1 - core) * 64, 64), pl.multiple_of(((1 - xh) * 2 + 1 - core) * 64, 64)]

    def piece(g, slot, rows):
        return hid.at[slot, pl.ds(rows, 64), pl.ds(GROUPS[g][0], GROUPS[g][1])]

    sent = []

    def push(src, dst, send_sem, recv_sem, to):
        cp = pltpu.make_async_remote_copy(src_ref=src, dst_ref=dst, send_sem=send_sem, recv_sem=recv_sem,
                                          device_id=to, device_id_type=MESH)
        cp.start()
        sent.append(cp)

    def arrived(dst, recv_sem, frm):
        pltpu.make_async_remote_copy(src_ref=dst, dst_ref=dst, send_sem=lsem.at[7], recv_sem=recv_sem,
                                     device_id=frm, device_id_type=MESH).wait_recv()

    def push_z(g, p, src, dst, to):
        push(piece(g, src, rows_of[p]), piece(g, dst, rows_of[p]), zs_sem.at[g, p, dst], rsem.at[g, p, dst], to)

    def forward(g, p, slot):
        once = GROUPS[g][2]
        if p == 0 and once and slot == 0:
            push(piece(g, 0, rows_of[0]), piece(g, 0, rows_of[0]), xs_sem.at[g, 0], rsem.at[g, 1, 0], across)
        if p == 0 or once:
            if slot in (0, 1, 3):
                push_z(g, p, slot, slot + 2 if slot else 1, down)
            if slot in (0, 2, 4):
                push_z(g, p, slot, slot + 2, up)
        if p == 0 and not once:
            push(piece(g, slot, rows_of[0]), piece(g, slot, rows_of[0]), xs_sem.at[g, slot], rsem.at[g, 1, slot],
                 across)
        push(piece(g, slot, rows_of[p]), piece(g, slot, rows_of[p]), bs_sem.at[g, p, slot], bsem.at[g, p, slot], sib)

    def got(g, p, slots):
        frm = across if p == 1 else up
        for slot in slots:
            arrived(piece(g, slot, rows_of[p]), rsem.at[g, p, slot], frm)
            forward(g, p, slot)
        if 5 in slots and (p == 0 or GROUPS[g][2]):
            push_z(g, p, 6 - core, 7, last)

    def sibling(phase, slots):
        for slot in slots:
            for g in PHASES[phase]:
                for p in (0, 1):
                    arrived(piece(g, slot, sib_rows[p]), bsem.at[g, p, slot], sib)

    def hidden(phase):
        for k in range(4):
            cols = pl.ds(phase * HALF + k * BLOCK, BLOCK)
            val = og[:, cols].astype(F32) * gelu_slope(pre[:, cols].astype(F32))
            hid[0, pl.ds(rows_of[0], 64), cols] = val.astype(BF)

    def dx_task(phase, first, n):
        cols = pl.ds(phase * HALF, HALF)
        val = mm(hid[pl.ds(first, n), :, cols].reshape(n * 256, HALF), wt[:, cols], NT)
        val = val.reshape(n, 256, BLOCK)
        if phase == 0:
            dxacc[pl.ds(first, n)] = val
        else:
            val = val + dxacc[pl.ds(first, n)]
            dxacc[pl.ds(first, n)] = val
            dxs[pl.ds(first, n)] = val.astype(BF)

    def dx_send(slots):
        for slot in slots:
            t = (z + DIST[slot]) % 8
            to_x, to_y = t // 4, t % 4
            j = (to_y + 4 - y) % 4

            @pl.when(j != 0)
            def _():
                pltpu.make_async_remote_copy(
                    src_ref=dxs.at[slot], dst_ref=dxr.at[to_x, j], send_sem=ds_sem.at[slot],
                    recv_sem=dsem.at[to_x, j], device_id=(r, xl * 4 + to_y), device_id_type=MESH).start()

    def dw_all(phase, k):
        cols = pl.ds(phase * HALF + k * 768, 768)
        dw[:, cols] = mm(tok[...], hid[:, :, cols].reshape(2048, 768))

    def dw_part(first, n, fresh):
        for k in range(2):
            cols = pl.ds(HALF + k * 768, 768)
            val = mm(tok[:, pl.ds(first * 256, n * 256)], hid[pl.ds(first, n), :, cols].reshape(n * 256, 768))
            dw[:, cols] = val if fresh else dw[:, cols] + val

    pending = []
    written = []

    def flush():
        for b in pending:
            cp = pltpu.make_async_copy(outs.at[:, :, pl.ds(b * BLOCK, BLOCK)],
                                       done_out.at[:, :, pl.ds(b * BLOCK, BLOCK)], os_sem.at[b])
            cp.start()
            written.append(cp)
        pending.clear()

    def stats(b):
        flush()
        cols = pl.ds(b * BLOCK, BLOCK)
        grad, left, right = statistics(dw[:, cols], scale)
        outs[0, :, cols] = grad
        outs[1, :, cols] = left
        outs[2, :, cols] = right
        pending.append(b)

    loads[0].wait()
    loads[1].wait()
    hidden(0)
    loads[2].wait()
    tok_own[...] = tok_raw[...].T
    pl.semaphore_wait(bar, len(peers))

    def own(phase):
        def over_x(g):
            push(piece(g, 0, rows_of[0]), piece(g, 0, rows_of[0]), xs_sem.at[g, 0], rsem.at[g, 1, 0], across)

        for g in ONCE[phase]:
            over_x(g)
        for g in EVERY[phase] + ONCE[phase]:
            push_z(g, 0, 0, 1, down)
            push_z(g, 0, 0, 2, up)
        for g in EVERY[phase]:
            over_x(g)
        for g in PHASES[phase]:
            push(piece(g, 0, rows_of[0]), piece(g, 0, rows_of[0]), bs_sem.at[g, 0, 0], bsem.at[g, 0, 0], sib)

    own(0)

    def tok_at(col):
        return tok.at[:, pl.ds(pl.multiple_of(slot_of((col + 8 - z) % 8) * 256, 256), 256)]

    push(tok_own, tok_at(c), ts_sem.at[0, 0], tsem.at[0, 0], xpeer)
    for j in (1, 2, 3):
        push(tok_own, tok_at(c), ts_sem.at[0, j], tsem.at[0, j], ypeer[j])
    keep = pltpu.make_async_copy(tok_own, tok_at(c), lsem.at[4])
    keep.start()
    hidden(1)
    loads[3].wait()

    def tok_relay():
        other = (1 - xl) * 4 + y
        arrived(tok_at(other), tsem.at[0, 0], xpeer)
        for j in (1, 2, 3):
            push(tok_at(other), tok_at(other), ts_sem.at[1, j], tsem.at[1, j], ypeer[j])

    def tok_wait():
        keep.wait()
        for j in (1, 2, 3):
            src_y = (y + 4 - j) % 4
            arrived(tok_at(xl * 4 + src_y), tsem.at[0, j], ypeer[j])
            arrived(tok_at((1 - xl) * 4 + src_y), tsem.at[1, j], ypeer[j])

    fill = [lambda: dw_all(0, 0), lambda: dw_all(0, 1)] + [functools.partial(stats, b) for b in range(4)]

    def filler(n=1):
        for _ in range(n):
            if fill:
                fill.pop(0)()

    def near(phase, s):
        first, n = LEVEL[s][0], len(LEVEL[s])
        sibling(phase, LEVEL[s])
        dx_task(phase, first, n)
        if (phase, s) == (0, 4):
            tok_wait()
        if phase:
            dw_part(first, n, s == 0)
            dx_send(LEVEL[s])

    def lazy(phase, s):
        if s == 4:
            for g in ONCE[phase]:
                got(g, 1, LEVEL[4])
        for g in EVERY[phase]:
            got(g, 1, LEVEL[s])

    order = [(phase, s) for phase in (0, 1) for s in range(5)]
    lazies, nears = list(order), list(order)

    def at(step):
        return step[0] * 4 + step[1]

    for step in order + [(1, s) for s in range(5, 5 + LAG + LAG2)]:
        phase, s = step
        if 1 <= s <= 4:
            if at(step) == OWN2:
                own(1)
            for g in EVERY[phase]:
                got(g, 0, LEVEL[s])
            for g in ONCE[phase]:
                got(g, 1, LEVEL[s - 1])
            for g in ONCE[phase]:
                got(g, 0, LEVEL[s])
        if s == 0:
            continue
        if at(step) == 2:
            tok_relay()
        while lazies and (at(lazies[0]) + LAG <= at(step)) and lazies[0][0] * 5 + lazies[0][1] <= phase * 5 + s:
            lazy(*lazies.pop(0))
        while nears and at(nears[0]) + LAG + LAG2 <= at(step) and (not lazies or nears[0] < lazies[0]):
            near(*nears.pop(0))
        if (0, 4) not in nears and s <= 4:
            filler(FILL_N)
    filler(9)

    rest = pltpu.make_async_copy(dw.at[:, pl.ds(early * BLOCK, (8 - early) * BLOCK)], rest_out, lsem.at[5])
    for b in range(4, early):
        stats(b)
    rest.start()

    def total(at_x):
        t = at_x * 4 + y
        val = dxacc[slot_of((t + 8 - z) % 8)]
        for j in (1, 2, 3):
            arrived(dxr.at[at_x, j], dsem.at[at_x, j], ypeer[j])
            val = val + dxr[at_x, j].astype(F32)
        return val

    xs[...] = total(1 - xl).astype(BF)
    flush()
    dxo_mine = total(xl)
    push(xs, xr, xsem.at[0], xsem.at[1], xpeer)
    arrived(xr, xsem.at[1], xpeer)
    dxo[...] = (dxo_mine + xr[...].astype(F32)).astype(BF)
    out = pltpu.make_async_copy(dxo, dx_out, lsem.at[6])
    out.start()
    for cp in sent:
        cp.wait_send()
    for slot in range(8):
        t = (z + DIST[slot]) % 8

        @pl.when((t % 4 + 4 - y) % 4 != 0)
        def _():
            pltpu.make_async_remote_copy(
                src_ref=dxs.at[slot], dst_ref=dxr.at[0, 1], send_sem=ds_sem.at[slot],
                recv_sem=dsem.at[0, 1], device_id=xpeer, device_id_type=MESH).wait_send()

    for cp in written:
        cp.wait()
    rest.wait()
    out.wait()


def finish(scale, early, done_in, rest_in, dx_in, gw_out, left_out, right_out, dx_out,
           done, rest, outs, dxv, isem, osem, rsem):
    late = 8 - early
    cps = [pltpu.make_async_copy(rest_in, rest, rsem), pltpu.make_async_copy(dx_in, dxv, isem.at[3])]
    cps += [pltpu.make_async_copy(done_in.at[i], done.at[i], isem.at[i]) for i in range(3)]
    for cp in cps:
        cp.start()
    hbm = (gw_out, left_out, right_out)
    res = []

    def put(src, dst, sem):
        cp = pltpu.make_async_copy(src, dst, sem)
        cp.start()
        res.append(cp)

    cps[0].wait()
    for k in range(late):
        cols = pl.ds(k * BLOCK, BLOCK)
        vals = statistics(rest[:, cols], scale)
        for i in range(3):
            outs[i, :, cols] = vals[i]
        if k == 0:
            for i in range(3):
                cps[2 + i].wait()
                put(done.at[i], hbm[i].at[:, pl.ds(0, early * BLOCK)], osem.at[8, i])
        for i in range(3):
            put(outs.at[i, :, cols], hbm[i].at[:, pl.ds((early + k) * BLOCK, BLOCK)], osem.at[k, i])
    cps[1].wait()
    put(dxv, dx_out, isem.at[4])
    for cp in res:
        cp.wait()


def on_device(tokens, weight, pre_act, out_grad):
    early = 8 - LATE
    scale = 1.0 / (BLOCK * 2048)
    anyspec = pl.BlockSpec(memory_space=pl.ANY)
    dma, vmem = pltpu.SemaphoreType.DMA, pltpu.VMEM
    done, rest, dx = pl.pallas_call(
        functools.partial(kernel, scale, early),
        out_shape=(
            jax.ShapeDtypeStruct((3, BLOCK, early * BLOCK), BF),
            jax.ShapeDtypeStruct((BLOCK, LATE * BLOCK), F32),
            jax.ShapeDtypeStruct((256, BLOCK), BF),
        ),
        in_specs=[anyspec] * 4,
        out_specs=(anyspec,) * 3,
        scratch_shapes=[
            vmem((8, 256, 3072), BF), vmem((BLOCK, 3072), BF), vmem((64, 3072), BF), vmem((64, 3072), BF),
            vmem((256, BLOCK), BF), vmem((BLOCK, 256), BF), vmem((BLOCK, 2048), BF),
            vmem((8, 256, BLOCK), F32), vmem((8, 256, BLOCK), BF), vmem((2, 4, 256, BLOCK), BF),
            vmem((256, BLOCK), BF), vmem((256, BLOCK), BF), vmem((256, BLOCK), BF),
            vmem((BLOCK, 3072), F32), vmem((3, BLOCK, early * BLOCK), BF),
            dma((8,)), dma((NB, 2, 8)), dma((NB, 2, 8)), dma((2, 4)), dma((2, 4)), dma((2,)),
            dma((NB, 2, 8)), dma((NB, 8)), dma((NB, 2, 8)), dma((2, 4)), dma((8,)), dma((8,)),
        ],
        compiler_params=pltpu.CompilerParams(collective_id=0, has_side_effects=True,
                                             vmem_limit_bytes=60 * 2**20),
        name="exchange",
    )(tokens, weight, pre_act, out_grad)
    full = jax.ShapeDtypeStruct((BLOCK, 3072), BF)
    gw, left, right, dx = pl.pallas_call(
        functools.partial(finish, scale, early),
        out_shape=(full, full, full, jax.ShapeDtypeStruct((256, BLOCK), BF)),
        in_specs=[anyspec] * 3,
        out_specs=(anyspec,) * 4,
        scratch_shapes=[
            vmem((3, BLOCK, early * BLOCK), BF), vmem((BLOCK, LATE * BLOCK), F32), vmem((3, BLOCK, LATE * BLOCK), BF),
            vmem((256, BLOCK), BF), dma((5,)), dma((9, 3)), dma,
        ],
        compiler_params=pltpu.CompilerParams(vmem_limit_bytes=60 * 2**20),
        name="finish",
    )(done, rest, dx)
    return dx, gw, left, right


def solution(mesh):
    specs = (P("col", "row"), P("row", "col"), P("row", "col"), P("row", "col"))
    return jax.shard_map(on_device, mesh=mesh, in_specs=specs, out_specs=specs, check_vma=False)
```

```python
import functools
import math

import jax
import jax.numpy as jnp
from jax import lax
from jax.experimental import pallas as pl
from jax.experimental.pallas import tpu as pltpu
from jax.sharding import PartitionSpec as P

MESH = pl.DeviceIdType.MESH
BF, F32 = jnp.bfloat16, jnp.float32
BLOCK = 384
LATE = 1
NT = (((1,), (1,)), ((), ()))
NN = (((1,), (0,)), ((), ()))
DIST = (0, 1, 7, 2, 6, 3, 5, 4)
W = 768
NB = 3072 // W
NONCE = (NB // 4, NB // 4)
GROUPS = tuple((g * W, W, g % (NB // 2) >= NB // 2 - NONCE[g // (NB // 2)]) for g in range(NB))
PHASES = (tuple(range(NB // 2)), tuple(range(NB // 2, NB)))
ONCE = tuple(tuple(g for g in ph if GROUPS[g][2]) for ph in PHASES)
EVERY = tuple(tuple(g for g in ph if not GROUPS[g][2]) for ph in PHASES)
LEVEL = ((0,), (1, 2), (3, 4), (5, 6), (7,))
LAG = 1
LAG2 = 1
OWN2 = 4
FILL_N = 2
HALF = 1536


def gelu_slope(value):
    coeff = math.sqrt(2.0 / math.pi)
    inner = coeff * (value + 0.044715 * value * value * value)
    tanh_u = jnp.tanh(inner)
    return 0.5 * (1.0 + tanh_u) + 0.5 * value * (1.0 - tanh_u * tanh_u) * coeff * (
        1.0 + 3.0 * 0.044715 * value * value
    )


def mm(a, b, dims=NN):
    return lax.dot_general(a, b, dims, preferred_element_type=F32)


def statistics(g, scale):
    hi = g.astype(BF)
    lo = (g - hi.astype(F32)).astype(BF)
    hi_t, lo_t = hi.T, lo.T
    a = mm(hi, lo_t)
    left = mm(hi, hi_t) + (a + a.T)
    b = mm(hi_t, lo)
    right = mm(hi_t, hi) + (b + b.T)
    return hi, (left * scale).astype(BF), (right * scale).astype(BF)


def slot_of(d):
    far = d // 5
    return (1 - far) * (2 * d - 1) + far * (16 - 2 * d) + (7 - d) // 7


def kernel(scale, early, tok_in, wt_in, pre_in, og_in, done_out, rest_out, dx_out,
           hid, wt, pre, og, tok_raw, tok_own, tok, dxacc, dxs, dxr, xs, xr, dxo, dw, outs,
           lsem, rsem, bsem, tsem, dsem, xsem, zs_sem, xs_sem, bs_sem, ts_sem, ds_sem, os_sem):
    r = lax.axis_index("row")
    c = lax.axis_index("col")
    core = r % 2
    xh = (r // 2) % 2
    z = r // 4
    xl = c // 4
    y = c % 4

    def row_id(zz, hh, cc):
        return (zz * 2 + hh) * 2 + cc

    sib = (row_id(z, xh, 1 - core), c)
    up = (row_id((z + 1) % 8, xh, core), c)
    down = (row_id((z + 7) % 8, xh, core), c)
    last = (row_id((z + 1 + 6 * core) % 8, xh, core), c)
    across = (row_id(z, 1 - xh, core), c)
    xpeer = (r, (1 - xl) * 4 + y)
    ypeer = [None] + [(r, xl * 4 + (y + j) % 4) for j in (1, 2, 3)]

    bar = pltpu.get_barrier_semaphore()
    peers = [sib, up, down, across, xpeer] + ypeer[1:]
    for peer in peers:
        pl.semaphore_signal(bar, inc=1, device_id=peer, device_id_type=MESH)

    loads = [
        pltpu.make_async_copy(pre_in, pre, lsem.at[0]),
        pltpu.make_async_copy(og_in, og, lsem.at[1]),
        pltpu.make_async_copy(tok_in, tok_raw, lsem.at[2]),
        pltpu.make_async_copy(wt_in, wt, lsem.at[3]),
    ]
    for cp in loads:
        cp.start()

    rows_of = [pl.multiple_of((xh * 2 + core) * 64, 64), pl.multiple_of(((1 - xh) * 2 + core) * 64, 64)]
    sib_rows = [pl.multiple_of((xh * 2 + 1 - core) * 64, 64), pl.multiple_of(((1 - xh) * 2 + 1 - core) * 64, 64)]

    def piece(g, slot, rows):
        return hid.at[slot, pl.ds(rows, 64), pl.ds(GROUPS[g][0], GROUPS[g][1])]

    sent = []

    def push(src, dst, send_sem, recv_sem, to):
        cp = pltpu.make_async_remote_copy(src_ref=src, dst_ref=dst, send_sem=send_sem, recv_sem=recv_sem,
                                          device_id=to, device_id_type=MESH)
        cp.start()
        sent.append(cp)

    def arrived(dst, recv_sem, frm):
        pltpu.make_async_remote_copy(src_ref=dst, dst_ref=dst, send_sem=lsem.at[7], recv_sem=recv_sem,
                                     device_id=frm, device_id_type=MESH).wait_recv()

    def push_z(g, p, src, dst, to):
        push(piece(g, src, rows_of[p]), piece(g, dst, rows_of[p]), zs_sem.at[g, p, dst], rsem.at[g, p, dst], to)

    def forward(g, p, slot):
        once = GROUPS[g][2]
        if p == 0 and once and slot == 0:
            push(piece(g, 0, rows_of[0]), piece(g, 0, rows_of[0]), xs_sem.at[g, 0], rsem.at[g, 1, 0], across)
        if p == 0 or once:
            if slot in (0, 1, 3):
                push_z(g, p, slot, slot + 2 if slot else 1, down)
            if slot in (0, 2, 4):
                push_z(g, p, slot, slot + 2, up)
        if p == 0 and not once:
            push(piece(g, slot, rows_of[0]), piece(g, slot, rows_of[0]), xs_sem.at[g, slot], rsem.at[g, 1, slot],
                 across)
        push(piece(g, slot, rows_of[p]), piece(g, slot, rows_of[p]), bs_sem.at[g, p, slot], bsem.at[g, p, slot], sib)

    def got(g, p, slots):
        frm = across if p == 1 else up
        for slot in slots:
            arrived(piece(g, slot, rows_of[p]), rsem.at[g, p, slot], frm)
            forward(g, p, slot)
        if 5 in slots and (p == 0 or GROUPS[g][2]):
            push_z(g, p, 6 - core, 7, last)

    def sibling(phase, slots):
        for slot in slots:
            for g in PHASES[phase]:
                for p in (0, 1):
                    arrived(piece(g, slot, sib_rows[p]), bsem.at[g, p, slot], sib)

    def hidden(phase):
        for k in range(4):
            cols = pl.ds(phase * HALF + k * BLOCK, BLOCK)
            val = og[:, cols].astype(F32) * gelu_slope(pre[:, cols].astype(F32))
            hid[0, pl.ds(rows_of[0], 64), cols] = val.astype(BF)

    def dx_task(phase, first, n):
        cols = pl.ds(phase * HALF, HALF)
        val = mm(hid[pl.ds(first, n), :, cols].reshape(n * 256, HALF), wt[:, cols], NT)
        val = val.reshape(n, 256, BLOCK)
        if phase == 0:
            dxacc[pl.ds(first, n)] = val
        else:
            val = val + dxacc[pl.ds(first, n)]
            dxacc[pl.ds(first, n)] = val
            dxs[pl.ds(first, n)] = val.astype(BF)

    def dx_send(slots):
        for slot in slots:
            t = (z + DIST[slot]) % 8
            to_x, to_y = t // 4, t % 4
            j = (to_y + 4 - y) % 4

            @pl.when(j != 0)
            def _():
                pltpu.make_async_remote_copy(
                    src_ref=dxs.at[slot], dst_ref=dxr.at[to_x, j], send_sem=ds_sem.at[slot],
                    recv_sem=dsem.at[to_x, j], device_id=(r, xl * 4 + to_y), device_id_type=MESH).start()

    def dw_all(phase, k):
        cols = pl.ds(phase * HALF + k * 768, 768)
        dw[:, cols] = mm(tok[...], hid[:, :, cols].reshape(2048, 768))

    def dw_part(first, n, fresh):
        for k in range(2):
            cols = pl.ds(HALF + k * 768, 768)
            val = mm(tok[:, pl.ds(first * 256, n * 256)], hid[pl.ds(first, n), :, cols].reshape(n * 256, 768))
            dw[:, cols] = val if fresh else dw[:, cols] + val

    pending = []
    written = []

    def flush():
        for b in pending:
            cp = pltpu.make_async_copy(outs.at[:, :, pl.ds(b * BLOCK, BLOCK)],
                                       done_out.at[:, :, pl.ds(b * BLOCK, BLOCK)], os_sem.at[b])
            cp.start()
            written.append(cp)
        pending.clear()

    def stats(b):
        flush()
        cols = pl.ds(b * BLOCK, BLOCK)
        grad, left, right = statistics(dw[:, cols], scale)
        outs[0, :, cols] = grad
        outs[1, :, cols] = left
        outs[2, :, cols] = right
        pending.append(b)

    loads[0].wait()
    loads[1].wait()
    hidden(0)
    loads[2].wait()
    tok_own[...] = tok_raw[...].T
    pl.semaphore_wait(bar, len(peers))

    def own(phase):
        def over_x(g):
            push(piece(g, 0, rows_of[0]), piece(g, 0, rows_of[0]), xs_sem.at[g, 0], rsem.at[g, 1, 0], across)

        for g in ONCE[phase]:
            over_x(g)
        for g in EVERY[phase] + ONCE[phase]:
            push_z(g, 0, 0, 1, down)
            push_z(g, 0, 0, 2, up)
        for g in EVERY[phase]:
            over_x(g)
        for g in PHASES[phase]:
            push(piece(g, 0, rows_of[0]), piece(g, 0, rows_of[0]), bs_sem.at[g, 0, 0], bsem.at[g, 0, 0], sib)

    own(0)

    def tok_at(col):
        return tok.at[:, pl.ds(pl.multiple_of(slot_of((col + 8 - z) % 8) * 256, 256), 256)]

    push(tok_own, tok_at(c), ts_sem.at[0, 0], tsem.at[0, 0], xpeer)
    for j in (1, 2, 3):
        push(tok_own, tok_at(c), ts_sem.at[0, j], tsem.at[0, j], ypeer[j])
    keep = pltpu.make_async_copy(tok_own, tok_at(c), lsem.at[4])
    keep.start()
    hidden(1)
    loads[3].wait()

    def tok_relay():
        other = (1 - xl) * 4 + y
        arrived(tok_at(other), tsem.at[0, 0], xpeer)
        for j in (1, 2, 3):
            push(tok_at(other), tok_at(other), ts_sem.at[1, j], tsem.at[1, j], ypeer[j])

    def tok_wait():
        keep.wait()
        for j in (1, 2, 3):
            src_y = (y + 4 - j) % 4
            arrived(tok_at(xl * 4 + src_y), tsem.at[0, j], ypeer[j])
            arrived(tok_at((1 - xl) * 4 + src_y), tsem.at[1, j], ypeer[j])

    fill = [lambda: dw_all(0, 0), lambda: dw_all(0, 1)] + [functools.partial(stats, b) for b in range(4)]

    def filler(n=1):
        for _ in range(n):
            if fill:
                fill.pop(0)()

    def near(phase, s):
        first, n = LEVEL[s][0], len(LEVEL[s])
        sibling(phase, LEVEL[s])
        dx_task(phase, first, n)
        if (phase, s) == (0, 4):
            tok_wait()
        if phase:
            dw_part(first, n, s == 0)
            dx_send(LEVEL[s])

    def lazy(phase, s):
        if s == 4:
            for g in ONCE[phase]:
                got(g, 1, LEVEL[4])
        for g in EVERY[phase]:
            got(g, 1, LEVEL[s])

    order = [(phase, s) for phase in (0, 1) for s in range(5)]
    lazies, nears = list(order), list(order)

    def at(step):
        return step[0] * 4 + step[1]

    for step in order + [(1, s) for s in range(5, 5 + LAG + LAG2)]:
        phase, s = step
        if 1 <= s <= 4:
            if at(step) == OWN2:
                own(1)
            for g in EVERY[phase]:
                got(g, 0, LEVEL[s])
            for g in ONCE[phase]:
                got(g, 1, LEVEL[s - 1])
            for g in ONCE[phase]:
                got(g, 0, LEVEL[s])
        if s == 0:
            continue
        if at(step) == 2:
            tok_relay()
        while lazies and (at(lazies[0]) + LAG <= at(step)) and lazies[0][0] * 5 + lazies[0][1] <= phase * 5 + s:
            lazy(*lazies.pop(0))
        while nears and at(nears[0]) + LAG + LAG2 <= at(step) and (not lazies or nears[0] < lazies[0]):
            near(*nears.pop(0))
        if (0, 4) not in nears and s <= 4:
            filler(FILL_N)
    filler(9)

    rest = pltpu.make_async_copy(dw.at[:, pl.ds(early * BLOCK, (8 - early) * BLOCK)], rest_out, lsem.at[5])
    for b in range(4, early):
        stats(b)
    rest.start()

    def total(at_x):
        t = at_x * 4 + y
        val = dxacc[slot_of((t + 8 - z) % 8)]
        for j in (1, 2, 3):
            arrived(dxr.at[at_x, j], dsem.at[at_x, j], ypeer[j])
            val = val + dxr[at_x, j].astype(F32)
        return val

    xs[...] = total(1 - xl).astype(BF)
    flush()
    dxo_mine = total(xl)
    push(xs, xr, xsem.at[0], xsem.at[1], xpeer)
    arrived(xr, xsem.at[1], xpeer)
    dxo[...] = (dxo_mine + xr[...].astype(F32)).astype(BF)
    out = pltpu.make_async_copy(dxo, dx_out, lsem.at[6])
    out.start()
    for cp in sent:
        cp.wait_send()
    for slot in range(8):
        t = (z + DIST[slot]) % 8

        @pl.when((t % 4 + 4 - y) % 4 != 0)
        def _():
            pltpu.make_async_remote_copy(
                src_ref=dxs.at[slot], dst_ref=dxr.at[0, 1], send_sem=ds_sem.at[slot],
                recv_sem=dsem.at[0, 1], device_id=xpeer, device_id_type=MESH).wait_send()

    for cp in written:
        cp.wait()
    rest.wait()
    out.wait()


def finish(scale, early, done_in, rest_in, dx_in, gw_out, left_out, right_out, dx_out,
           done, rest, outs, dxv, isem, osem, rsem):
    late = 8 - early
    cps = [pltpu.make_async_copy(rest_in, rest, rsem), pltpu.make_async_copy(dx_in, dxv, isem.at[3])]
    cps += [pltpu.make_async_copy(done_in.at[i], done.at[i], isem.at[i]) for i in range(3)]
    for cp in cps:
        cp.start()
    hbm = (gw_out, left_out, right_out)
    res = []

    def put(src, dst, sem):
        cp = pltpu.make_async_copy(src, dst, sem)
        cp.start()
        res.append(cp)

    cps[0].wait()
    for k in range(late):
        cols = pl.ds(k * BLOCK, BLOCK)
        vals = statistics(rest[:, cols], scale)
        for i in range(3):
            outs[i, :, cols] = vals[i]
        if k == 0:
            for i in range(3):
                cps[2 + i].wait()
                put(done.at[i], hbm[i].at[:, pl.ds(0, early * BLOCK)], osem.at[8, i])
        for i in range(3):
            put(outs.at[i, :, cols], hbm[i].at[:, pl.ds((early + k) * BLOCK, BLOCK)], osem.at[k, i])
    cps[1].wait()
    put(dxv, dx_out, isem.at[4])
    for cp in res:
        cp.wait()


def on_device(tokens, weight, pre_act, out_grad):
    early = 8 - LATE
    scale = 1.0 / (BLOCK * 2048)
    anyspec = pl.BlockSpec(memory_space=pl.ANY)
    dma, vmem = pltpu.SemaphoreType.DMA, pltpu.VMEM
    done, rest, dx = pl.pallas_call(
        functools.partial(kernel, scale, early),
        out_shape=(
            jax.ShapeDtypeStruct((3, BLOCK, early * BLOCK), BF),
            jax.ShapeDtypeStruct((BLOCK, LATE * BLOCK), F32),
            jax.ShapeDtypeStruct((256, BLOCK), BF),
        ),
        in_specs=[anyspec] * 4,
        out_specs=(anyspec,) * 3,
        scratch_shapes=[
            vmem((8, 256, 3072), BF), vmem((BLOCK, 3072), BF), vmem((64, 3072), BF), vmem((64, 3072), BF),
            vmem((256, BLOCK), BF), vmem((BLOCK, 256), BF), vmem((BLOCK, 2048), BF),
            vmem((8, 256, BLOCK), F32), vmem((8, 256, BLOCK), BF), vmem((2, 4, 256, BLOCK), BF),
            vmem((256, BLOCK), BF), vmem((256, BLOCK), BF), vmem((256, BLOCK), BF),
            vmem((BLOCK, 3072), F32), vmem((3, BLOCK, early * BLOCK), BF),
            dma((8,)), dma((NB, 2, 8)), dma((NB, 2, 8)), dma((2, 4)), dma((2, 4)), dma((2,)),
            dma((NB, 2, 8)), dma((NB, 8)), dma((NB, 2, 8)), dma((2, 4)), dma((8,)), dma((8,)),
        ],
        compiler_params=pltpu.CompilerParams(collective_id=0, has_side_effects=True,
                                             vmem_limit_bytes=60 * 2**20),
        name="exchange",
    )(tokens, weight, pre_act, out_grad)
    full = jax.ShapeDtypeStruct((BLOCK, 3072), BF)
    gw, left, right, dx = pl.pallas_call(
        functools.partial(finish, scale, early),
        out_shape=(full, full, full, jax.ShapeDtypeStruct((256, BLOCK), BF)),
        in_specs=[anyspec] * 3,
        out_specs=(anyspec,) * 4,
        scratch_shapes=[
            vmem((3, BLOCK, early * BLOCK), BF), vmem((BLOCK, LATE * BLOCK), F32), vmem((3, BLOCK, LATE * BLOCK), BF),
            vmem((256, BLOCK), BF), dma((5,)), dma((9, 3)), dma,
        ],
        compiler_params=pltpu.CompilerParams(vmem_limit_bytes=60 * 2**20),
        name="finish",
    )(done, rest, dx)
    return dx, gw, left, right


def solution(mesh):
    specs = (P("col", "row"), P("row", "col"), P("row", "col"), P("row", "col"))
    return jax.shard_map(on_device, mesh=mesh, in_specs=specs, out_specs=specs, check_vma=False)
```
